32 devices in a mesh: dp: 4 (over x, core), expert: 8 (over z, y).
Axes of the slice: x: 2, y: 2, z: 4, core: 2. Of those that a mesh axis runs over, the one named last changes fastest.
Arguments:
- tokens: bfloat16 [4096, 4096], P(('dp', 'expert')), may hold values from -6 to 6
- expert_ids: int32 [4096, 2], P(('dp', 'expert')), may hold values from 0 to 7, as said below
- gate_codes: int32 [4096, 2], P(('dp', 'expert')), may hold values from 1 to 64
- w_gate: bfloat16 [8, 4096, 768], P('expert'), may hold values from -0.09375 to 0.09375
- w_up: bfloat16 [8, 4096, 768], P('expert'), may hold values from -0.09375 to 0.09375
- w_down: bfloat16 [8, 768, 4096], P('expert'), may hold values from -0.21875 to 0.21875
- out_grad: bfloat16 [4096, 4096], P(('dp', 'expert')), may hold values from -6 to 6
Outputs:
- layer_out: bfloat16 [4096, 4096], P(('dp', 'expert'))
- tokens_grad: bfloat16 [4096, 4096], P(('dp', 'expert'))
- gate_weight_grad: bfloat16 [8, 4096, 768], P('expert', 'dp')
- up_weight_grad: bfloat16 [8, 4096, 768], P('expert', 'dp')
- down_weight_grad: bfloat16 [8, 768, 4096], P('expert', None, 'dp')
The draws below stay inside these ranges and needn't reach their ends.
Inputs may be any that keep to these rules, and one draw needn't show every extreme that they name: `expert_ids`: each token names 2 different experts. In the rows of one device no expert is named more than 48 times, and in every draw one and the same expert is named exactly 48 times by the rows of every device.
All inputs are finite; a program needn't handle non-finite values.
Results may differ from the reference program's by a relative error of at most 0.009.
Values may be sent and summed in bfloat16 or wider, within the bound.
A program may use at most 192 MiB of HBM per device.

```python
import jax
import jax.numpy as jnp
from jax import lax

D = 4096
HID = 768
TOPK = 2
TOK_DEV = 128
EXPERTS = 8
CAP = 48
TOKENS = 4096


def route_block(block_key, hot_expert):
    key_order, key_weight, key_tokens, key_shift = jax.random.split(block_key, 4)
    pair_count = TOK_DEV * TOPK
    spare_slots = pair_count - CAP
    shuffled = jax.random.permutation(key_order, EXPERTS).astype(jnp.int32)
    expert_range = jnp.arange(EXPERTS, dtype=jnp.int32)
    sort_score = jnp.where(shuffled == hot_expert, -1, expert_range)
    ordering = shuffled[jnp.argsort(sort_score, stable=True)]
    range_weight = jax.random.randint(key_weight, (EXPERTS,), 2, 4).astype(jnp.int32)
    range_weight = range_weight.at[0].set(0)
    running = jnp.cumsum(range_weight)
    bounds = CAP + spare_slots * running // running[-1]
    slot_index = jnp.arange(pair_count, dtype=jnp.int32)
    slot_shift = jax.random.randint(key_shift, (), 0, pair_count).astype(jnp.int32)
    rotated = (slot_index + slot_shift) % pair_count
    position = jnp.sum((rotated[:, None] >= bounds[None, :]).astype(jnp.int32), axis=1)
    chosen = ordering[position]
    pair_table = chosen.reshape(TOPK, TOK_DEV).T
    token_order = jax.random.permutation(key_tokens, TOK_DEV).astype(jnp.int32)
    inverse = jnp.argsort(token_order, stable=True)
    return pair_table[inverse]


def draw_expert_ids(key, part):
    key_hot, key_blocks = jax.random.split(jax.random.fold_in(key, 17))
    hot_expert = jax.random.randint(key_hot, (), 0, EXPERTS).astype(jnp.int32)
    block_keys = jax.random.split(key_blocks, TOKENS // TOK_DEV)
    tables = jax.vmap(route_block, in_axes=(0, None))(block_keys, hot_expert)
    return tables.reshape(TOKENS, TOPK).astype(jnp.int32)


def touch_ends(values, rng, smallest, high):
    longest = values.shape.index(max(values.shape))
    spots = []
    for shift in (0, 1):
        where = [jax.random.randint(jax.random.fold_in(rng, axis), (), 0, length) for axis, length in enumerate(values.shape)]
        where[longest] = (where[longest] + shift) % values.shape[longest]
        spots.append(tuple(where))
    return values.at[spots[0]].set(smallest).at[spots[1]].set(high)


def levels(own_key, shape, shards, low, top_value):
    gain, own = 1.0, jax.random.fold_in(own_key, 6)
    for dim, parts in shards:
        draws = jnp.exp(jax.random.uniform(jax.random.fold_in(own, dim), (parts,), jnp.float32, low / len(shards), top_value / len(shards)))
        gain = gain * jnp.repeat(draws, shape[dim] // parts).reshape([-1 if axis == dim else 1 for axis in range(len(shape))])
    return gain


def centred(key, shape, scale, most, pieces=(), held_as=jnp.bfloat16):
    drawn = scale * jax.random.normal(key, shape, jnp.float32)
    if pieces:
        drawn = drawn * levels(key, shape, pieces, -0.22, 0.18)
    return jnp.clip(drawn, -most, most).astype(held_as)


def setup_inputs(seed: int = 0) -> dict:
    key_of = jax.random.split(jax.random.key(seed), 8)
    tokens = centred(key_of[0], (TOKENS, D), 1.0, 6.0, ((0, 32),))
    expert_ids = draw_expert_ids(jax.random.fold_in(key_of[7], 71), 0)
    gate_codes = touch_ends(jax.random.randint(key_of[2], (TOKENS, TOPK), 1, 65), jax.random.fold_in(key_of[2], 1), 1, 64).astype(jnp.int32)
    w_gate = centred(key_of[3], (EXPERTS, D, HID), D ** -0.5, 0.09375, ((0, 8),))
    w_up = centred(key_of[4], (EXPERTS, D, HID), D ** -0.5, 0.09375, ((0, 8),))
    w_down = centred(key_of[5], (EXPERTS, HID, D), HID ** -0.5, 0.21875, ((0, 8),))
    out_grad = centred(key_of[6], (TOKENS, D), 1.0, 6.0, ((0, 32),))
    return dict(tokens=tokens, expert_ids=expert_ids, gate_codes=gate_codes, w_gate=w_gate, w_up=w_up, w_down=w_down, out_grad=out_grad)


def slot_targets(block_ids):
    flat_ids = block_ids.reshape(-1)
    one_hot = (flat_ids[:, None] == jnp.arange(EXPERTS, dtype=jnp.int32)[None, :]).astype(jnp.int32)
    earlier = jnp.cumsum(one_hot, axis=0) - one_hot
    slot_ranks = jnp.sum(earlier * one_hot, axis=1)
    return (flat_ids * CAP + slot_ranks).astype(jnp.int32)


def owner_table(targets):
    pair_count = targets.shape[0]
    return jnp.full((EXPERTS * CAP,), -1, jnp.int32).at[targets].set(jnp.arange(pair_count, dtype=jnp.int32))


def group_sums(left_rows, right_rows, group_count):
    left_rows = left_rows.reshape(group_count, EXPERTS * CAP, left_rows.shape[-1]).astype(jnp.float32)
    right_rows = right_rows.reshape(group_count, EXPERTS * CAP, right_rows.shape[-1]).astype(jnp.float32)
    partials = jnp.einsum("gri,grj->gij", left_rows, right_rows)
    partials = lax.optimization_barrier(partials.astype(jnp.bfloat16)).astype(jnp.float32)
    return jnp.sum(partials, axis=0).astype(jnp.bfloat16)


def reference(tokens, expert_ids, gate_codes, w_gate, w_up, w_down, out_grad):
    block_count = TOKENS // TOK_DEV
    group_count = block_count // EXPERTS
    pair_count = TOK_DEV * TOPK
    token_blocks = tokens.reshape(block_count, TOK_DEV, D)
    grad_blocks = out_grad.reshape(block_count, TOK_DEV, D)
    gate_blocks = gate_codes.astype(jnp.float32).reshape(block_count, pair_count) / 64.0
    targets = jax.vmap(slot_targets)(expert_ids.reshape(block_count, TOK_DEV, TOPK))
    owners = jax.vmap(owner_table)(targets).reshape(block_count, EXPERTS, CAP)
    block_index = jnp.arange(block_count, dtype=jnp.int32)[:, None]
    contract = (((1,), (1,)), ((), ()))

    def one_expert(carry, expert):
        out_total, grad_total = carry
        slot_pairs = lax.dynamic_index_in_dim(owners, expert, 1, keepdims=False)
        is_live = slot_pairs >= 0
        safe_pair = jnp.maximum(slot_pairs, 0)
        token_pos = safe_pair // TOPK
        pair_gains = jnp.where(is_live, jnp.take_along_axis(gate_blocks, safe_pair, axis=1), 0.0)
        gate_matrix = lax.dynamic_index_in_dim(w_gate, expert, 0, keepdims=False)
        up_matrix = lax.dynamic_index_in_dim(w_up, expert, 0, keepdims=False)
        down_matrix = lax.dynamic_index_in_dim(w_down, expert, 0, keepdims=False)
        picked = token_blocks[block_index, token_pos]
        picked = jnp.where(is_live[..., None], picked, jnp.zeros((), jnp.bfloat16)).reshape(block_count * CAP, D)
        pre_gate = jnp.dot(picked, gate_matrix, preferred_element_type=jnp.float32)
        pre_up = jnp.dot(picked, up_matrix, preferred_element_type=jnp.float32)
        sigmoid_gate = jax.nn.sigmoid(pre_gate)
        silu_gate = pre_gate * sigmoid_gate
        hidden = (silu_gate * pre_up).astype(jnp.bfloat16)
        expert_out = jnp.dot(hidden, down_matrix, preferred_element_type=jnp.float32).astype(jnp.bfloat16)
        expert_out = expert_out.reshape(block_count, CAP, D)
        upstream = grad_blocks[block_index, token_pos]
        pair_grad = (pair_gains[..., None] * upstream.astype(jnp.float32)).astype(jnp.bfloat16)
        pair_grad = pair_grad.reshape(block_count * CAP, D)
        hidden_grad = lax.dot_general(pair_grad, down_matrix, contract, preferred_element_type=jnp.float32)
        gate_pre_grad = (hidden_grad * pre_up * sigmoid_gate * (1.0 + pre_gate * (1.0 - sigmoid_gate))).astype(jnp.bfloat16)
        up_pre_grad = (hidden_grad * silu_gate).astype(jnp.bfloat16)
        input_grad = lax.dot_general(gate_pre_grad, gate_matrix, contract, preferred_element_type=jnp.float32)
        input_grad = input_grad + lax.dot_general(up_pre_grad, up_matrix, contract, preferred_element_type=jnp.float32)
        input_grad = input_grad.astype(jnp.bfloat16).reshape(block_count, CAP, D)
        weighted = pair_gains[..., None] * expert_out.astype(jnp.float32)
        out_total = out_total.at[block_index, token_pos].add(weighted)
        masked_grad = jnp.where(is_live[..., None], input_grad.astype(jnp.float32), 0.0)
        grad_total = grad_total.at[block_index, token_pos].add(masked_grad)
        gate_sum = group_sums(picked, gate_pre_grad, group_count)
        up_sum = group_sums(picked, up_pre_grad, group_count)
        down_sum = group_sums(hidden, pair_grad, group_count)
        return (out_total, grad_total), (gate_sum, up_sum, down_sum)

    start_total = jnp.zeros((block_count, TOK_DEV, D), jnp.float32)
    carried, stacked = lax.scan(one_expert, (start_total, start_total), jnp.arange(EXPERTS, dtype=jnp.int32))
    layer_out = carried[0].astype(jnp.bfloat16).reshape(TOKENS, D)
    tokens_grad = carried[1].astype(jnp.bfloat16).reshape(TOKENS, D)
    return (layer_out, tokens_grad, stacked[0], stacked[1], stacked[2])
```

```python
import jax
import jax.numpy as jnp
from jax import lax
from jax.sharding import PartitionSpec as P


def selection(expert_ids, gate_codes, experts, capacity):
    tok_count = expert_ids.shape[0]
    expert_range = jnp.arange(experts, dtype=jnp.int32)
    named = expert_ids[:, :, None] == expert_range[None, None, :]
    chosen = jnp.any(named, axis=1).T
    gates = jnp.sum(jnp.where(named, gate_codes[:, :, None], 0), axis=1).T
    gates = gates.astype(jnp.float32) * (1.0 / 64.0)
    earlier = (
        jnp.arange(tok_count, dtype=jnp.int32)[:, None] < jnp.arange(tok_count, dtype=jnp.int32)[None, :]
    )
    ranks = jnp.dot(
        chosen.astype(jnp.bfloat16), earlier.astype(jnp.bfloat16), preferred_element_type=jnp.float32
    ).astype(jnp.int32)
    slots = jnp.where(chosen, ranks, -1)
    hit = slots[:, None, :] == jnp.arange(capacity, dtype=jnp.int32)[None, :, None]
    sel = hit.astype(jnp.bfloat16).reshape(experts * capacity, tok_count)
    sel_gate = jnp.where(hit, gates[:, None, :], 0.0).astype(jnp.bfloat16)
    return sel, sel_gate.reshape(experts * capacity, tok_count)


def swap_columns(rows, groups, me):
    width = rows.shape[1] // groups
    parts = [lax.dynamic_slice_in_dim(rows, me * width, width, axis=1)]
    for shift in range(1, groups):
        target = lax.rem(me + shift, groups)
        piece = lax.dynamic_slice_in_dim(rows, target * width, width, axis=1)
        parts.append(
            lax.ppermute(piece, "dp", [(i, (i + shift) % groups) for i in range(groups)])
        )
    return parts


def per_device(tokens, expert_ids, gate_codes, w_gate, w_up, w_down, out_grad):
    experts = lax.axis_size("expert")
    groups = lax.axis_size("dp")
    me = lax.axis_index("dp")
    tok_count, model_width = tokens.shape
    pair_count = tok_count * expert_ids.shape[1]
    capacity = 3 * pair_count // (2 * experts)
    f32 = jnp.float32
    bf16 = jnp.bfloat16
    sel, sel_gate = selection(expert_ids, gate_codes, experts, capacity)
    gate_matrix, up_matrix, down_matrix = w_gate[0], w_up[0], w_down[0]
    hidden_units = gate_matrix.shape[1]
    contract = (((1,), (1,)), ((), ()))
    contract_rows = (((0,), (0,)), ((), ()))

    def exchange(rows):
        rows = rows.reshape(experts, capacity, model_width)
        rows = lax.all_to_all(rows, "expert", split_axis=0, concat_axis=0, tiled=True)
        return rows.reshape(experts * capacity, model_width)

    arrived = exchange(jnp.dot(sel, tokens, preferred_element_type=f32).astype(bf16))
    incoming = exchange(jnp.dot(sel_gate, out_grad, preferred_element_type=f32).astype(bf16))
    pre_gate = jnp.dot(arrived, gate_matrix, preferred_element_type=f32)
    pre_up = jnp.dot(arrived, up_matrix, preferred_element_type=f32)
    sigmoid_gate = jax.nn.sigmoid(pre_gate)
    silu_gate = pre_gate * sigmoid_gate
    hidden = (silu_gate * pre_up).astype(bf16)
    produced = jnp.dot(hidden, down_matrix, preferred_element_type=f32).astype(bf16)
    returned = exchange(produced)
    layer_out = lax.dot_general(sel_gate, returned, contract_rows, preferred_element_type=f32)

    arrived_parts = swap_columns(arrived, groups, me)
    incoming_parts = swap_columns(incoming, groups, me)

    hidden_grad = lax.dot_general(incoming, down_matrix, contract, preferred_element_type=f32)
    gate_pre_grad = (
        hidden_grad * pre_up * sigmoid_gate * (1.0 + pre_gate * (1.0 - sigmoid_gate))
    ).astype(bf16)
    up_pre_grad = (hidden_grad * silu_gate).astype(bf16)
    input_grad = lax.dot_general(gate_pre_grad, gate_matrix, contract, preferred_element_type=f32)
    input_grad = input_grad + lax.dot_general(
        up_pre_grad, up_matrix, contract, preferred_element_type=f32
    )
    returned_grad = exchange(input_grad.astype(bf16))
    tokens_grad = lax.dot_general(sel, returned_grad, contract_rows, preferred_element_type=f32)

    factors = jnp.concatenate([gate_pre_grad, up_pre_grad, hidden], axis=0)
    gathered = lax.all_gather(factors, "dp", axis=0, tiled=False)
    rows = experts * capacity

    gate_sum = up_sum = down_sum = 0.0
    for shift in range(groups):
        source = lax.rem(me - shift + groups, groups)
        factor = factors if shift == 0 else lax.dynamic_index_in_dim(gathered, source, 0, keepdims=False)
        tok, grad = arrived_parts[shift], incoming_parts[shift]
        gate_sum += lax.dot_general(tok, factor[:rows], contract_rows, preferred_element_type=f32)
        up_sum += lax.dot_general(
            tok, factor[rows : 2 * rows], contract_rows, preferred_element_type=f32
        )
        down_sum += lax.dot_general(
            factor[2 * rows :], grad, contract_rows, preferred_element_type=f32
        )
    return (
        layer_out.astype(bf16),
        tokens_grad.astype(bf16),
        gate_sum.astype(bf16)[None],
        up_sum.astype(bf16)[None],
        down_sum.astype(bf16)[None],
    )


def solution(mesh):
    placed = (
        P(("dp", "expert"), None),
        P(("dp", "expert"), None),
        P(("dp", "expert"), None),
        P("expert", None, None),
        P("expert", None, None),
        P("expert", None, None),
        P(("dp", "expert"), None),
    )
    return jax.shard_map(
        per_device,
        mesh=mesh,
        in_specs=placed,
        out_specs=(
            P(("dp", "expert"), None),
            P(("dp", "expert"), None),
            P("expert", "dp", None),
            P("expert", "dp", None),
            P("expert", None, "dp"),
        ),
        check_vma=False,
    )
```

```python
import functools

import jax
import jax.numpy as jnp
from jax import lax
from jax.experimental import pallas as pl
from jax.experimental.pallas import tpu as pltpu
from jax.sharding import PartitionSpec as P

F32 = jnp.float32
BF16 = jnp.bfloat16
CHUNKS = 4
CONTRACT = (((1,), (1,)), ((), ()))


def positions(half):
    me = lax.axis_index("expert")
    side = me // half
    local = me - side * half
    base = side * half
    partner = (1 - side) * half + local
    return me, side, local, base, partner


def meet(half, local, base, partner):
    barrier = pltpu.get_barrier_semaphore()
    for j in range(1, half):
        pl.semaphore_signal(barrier, inc=1, device_id={"expert": base + lax.rem(local + j, half)})
    pl.semaphore_signal(barrier, inc=1, device_id={"expert": partner})
    pl.semaphore_wait(barrier, half)


def remote(src, dst, send, recv, peer):
    return pltpu.make_async_remote_copy(
        src_ref=src, dst_ref=dst, send_sem=send, recv_sem=recv, device_id={"expert": peer}
    )


def dispatch_kernel(
    half, cap,
    sel, sel_t, tokens, out_grad, w_gate, w_up, w_down,
    arrived, incoming, hidden, gate_pre_grad, up_pre_grad, far_sel_t,
    far_sel, far_src, stage, pre_gate, pre_up, hidden_grad, vgate, vup, vdown,
    load_sem, sel_send, sel_recv, far_send, far_recv, near_send, near_recv,
):
    me, side, local, base, partner = positions(half)
    width = tokens.shape[1] // CHUNKS
    steps = 2 * CHUNKS
    loads = [
        pltpu.make_async_copy(a, b, load_sem.at[i])
        for i, (a, b) in enumerate(((w_gate, vgate), (w_up, vup), (w_down, vdown)))
    ]
    meet(half, local, base, partner)
    sources = (tokens, out_grad)
    landed = (arrived, incoming)
    sel_copies = [
        remote(sel.at[1 - side], far_sel, sel_send.at[0], sel_recv.at[0], partner),
        remote(sel_t.at[1 - side], far_sel_t, sel_send.at[1], sel_recv.at[1], partner),
    ]
    sel_copies[0].start()

    def columns(q):
        return pl.ds((q % CHUNKS) * width, width)

    far = [
        remote(sources[q // CHUNKS].at[:, columns(q)], far_src.at[q], far_send.at[q], far_recv.at[q], partner)
        for q in range(steps)
    ]
    started = [[] for _ in range(steps)]

    def rows_of(index):
        return pl.ds(pl.multiple_of(index * cap, 16), cap)

    def spread(q, kind, matrix, values, owner):
        part = q // CHUNKS
        slots = jnp.dot(matrix, values, preferred_element_type=F32).astype(BF16)
        stage[q, kind] = slots
        for j in range(1, half):
            peer = lax.rem(local + j, half)
            copy = remote(
                stage.at[q, kind, rows_of(peer)],
                landed[part].at[rows_of(owner), columns(q)],
                near_send.at[q, kind, j - 1],
                near_recv.at[q, kind, j - 1],
                base + peer,
            )
            copy.start()
            started[q].append(copy)
        landed[part][rows_of(owner), columns(q)] = stage[q, kind, rows_of(local)]

    far[0].start()
    for load in loads:
        load.start()
    for s in range(steps + 2):
        if s + 1 < steps:
            far[s + 1].start()
        if s == 0:
            sel_copies[1].start()
        if s < steps:
            part = s // CHUNKS
            spread(s, 0, sel[side, part], sources[part][:, columns(s)], me)
        if 1 <= s <= steps:
            q = s - 1
            if q == 0:
                sel_copies[0].wait_recv()
            far[q].wait_recv()
            spread(q, 1, far_sel[q // CHUNKS], far_src[q], partner)
        if s >= 2:
            q = s - 2
            for copy in started[q]:
                copy.wait_recv()
            part = q // CHUNKS
            rows = landed[part][:, columns(q)]
            if q == 0:
                loads[0].wait()
                loads[1].wait()
            if q == CHUNKS:
                loads[2].wait()
            if part == 0:
                for total, matrix in ((pre_gate, vgate), (pre_up, vup)):
                    term = jnp.dot(rows, matrix[columns(q), :], preferred_element_type=F32)
                    total[...] = term if q == 0 else total[...] + term
            else:
                term = lax.dot_general(rows, vdown[:, columns(q)], CONTRACT, preferred_element_type=F32)
                hidden_grad[...] = term if q == CHUNKS else hidden_grad[...] + term
    block = cap
    for start in range(0, pre_gate.shape[0], block):
        at = pl.ds(start, block)
        gate, up, grad = pre_gate[at, :], pre_up[at, :], hidden_grad[at, :]
        sigmoid = jax.nn.sigmoid(gate)
        silu = gate * sigmoid
        hidden[at, :] = (silu * up).astype(BF16)
        gate_pre_grad[at, :] = (grad * up * sigmoid * (1.0 + gate * (1.0 - sigmoid))).astype(BF16)
        up_pre_grad[at, :] = (grad * silu).astype(BF16)
    sel_copies[1].wait_recv()
    for copy in sel_copies + far:
        copy.wait_send()
    for q in range(steps):
        for copy in started[q]:
            copy.wait_send()


def return_kernel(
    half, cap,
    sel_t, far_sel_t, hidden, gate_pre_grad, up_pre_grad, w_gate, w_up, w_down,
    layer_out, tokens_grad,
    stage, back, part_send, part_recv, vgate, vup, vdown,
    load_sem, far_send, far_recv, near_send, near_recv,
):
    me, side, local, base, partner = positions(half)
    width = layer_out.shape[1] // CHUNKS
    steps = 2 * CHUNKS
    rows = half * cap
    loads = [
        pltpu.make_async_copy(a, b, load_sem.at[i])
        for i, (a, b) in enumerate(((w_down, vdown), (w_gate, vgate), (w_up, vup)))
    ]
    for load in loads:
        load.start()
    meet(half, local, base, partner)
    outs = (layer_out, tokens_grad)

    def columns(q):
        return pl.ds((q % CHUNKS) * width, width)

    def rows_of(index):
        return pl.ds(pl.multiple_of(index * cap, 16), cap)

    far = [
        remote(part_send_ref, part_recv_ref, far_send.at[q], far_recv.at[q], partner)
        for q, (part_send_ref, part_recv_ref) in enumerate(
            (part_send.at[q], part_recv.at[q]) for q in range(steps)
        )
    ]
    started = [([], []) for _ in range(steps)]
    for s in range(steps + 2):
        if s < steps:
            if s == 0:
                loads[0].wait()
            if s == CHUNKS:
                loads[1].wait()
                loads[2].wait()
            if s < CHUNKS:
                made = jnp.dot(hidden[...], vdown[:, columns(s)], preferred_element_type=F32)
            else:
                made = lax.dot_general(gate_pre_grad[...], vgate[columns(s), :], CONTRACT, preferred_element_type=F32)
                made = made + lax.dot_general(
                    up_pre_grad[...], vup[columns(s), :], CONTRACT, preferred_element_type=F32
                )
            stage[s] = made.astype(BF16)
            for kind in (1, 0):
                first = base if kind == 0 else half - base
                for j in range(1, half):
                    peer = lax.rem(local + j, half)
                    copy = remote(
                        stage.at[s, rows_of(first + peer)],
                        back.at[s, kind, rows_of(local)],
                        near_send.at[s, kind, j - 1],
                        near_recv.at[s, kind, j - 1],
                        base + peer,
                    )
                    copy.start()
                    started[s][kind].append(copy)
                back[s, kind, rows_of(local)] = stage[s, rows_of(first + local)]
        if 1 <= s <= steps:
            q = s - 1
            for copy in started[q][1]:
                copy.wait_recv()
            part_send[q] = jnp.dot(
                far_sel_t[1 - q // CHUNKS], back[q, 1], preferred_element_type=F32
            ).astype(BF16)
            far[q].start()
        if s >= 2:
            q = s - 2
            for copy in started[q][0]:
                copy.wait_recv()
            near = jnp.dot(sel_t[side, 1 - q // CHUNKS], back[q, 0], preferred_element_type=F32)
            far[q].wait_recv()
            outs[q // CHUNKS][:, columns(q)] = (near + part_recv[q].astype(F32)).astype(BF16)
    for q in range(steps):
        far[q].wait_send()
        for copies in started[q]:
            for copy in copies:
                copy.wait_send()


def selection(expert_ids, gate_codes, experts, capacity):
    tok_count = expert_ids.shape[0]
    expert_range = jnp.arange(experts, dtype=jnp.int32)
    named = expert_ids[:, :, None] == expert_range[None, None, :]
    chosen = jnp.any(named, axis=1).T
    gates = jnp.sum(jnp.where(named, gate_codes[:, :, None], 0), axis=1).T
    gates = gates.astype(jnp.float32) * (1.0 / 64.0)
    earlier = (
        jnp.arange(tok_count, dtype=jnp.int32)[:, None] < jnp.arange(tok_count, dtype=jnp.int32)[None, :]
    )
    ranks = jnp.dot(
        chosen.astype(jnp.bfloat16), earlier.astype(jnp.bfloat16), preferred_element_type=jnp.float32
    ).astype(jnp.int32)
    slots = jnp.where(chosen, ranks, -1)
    hit = slots[:, None, :] == jnp.arange(capacity, dtype=jnp.int32)[None, :, None]
    sel = hit.astype(jnp.bfloat16).reshape(experts * capacity, tok_count)
    sel_gate = jnp.where(hit, gates[:, None, :], 0.0).astype(jnp.bfloat16)
    return sel, sel_gate.reshape(experts * capacity, tok_count)


def swap_columns(rows, groups, me):
    width = rows.shape[1] // groups
    parts = [lax.dynamic_slice_in_dim(rows, me * width, width, axis=1)]
    for shift in range(1, groups):
        target = lax.rem(me + shift, groups)
        piece = lax.dynamic_slice_in_dim(rows, target * width, width, axis=1)
        parts.append(
            lax.ppermute(piece, "dp", [(i, (i + shift) % groups) for i in range(groups)])
        )
    return parts


def per_device(tokens, expert_ids, gate_codes, w_gate, w_up, w_down, out_grad):
    experts = lax.axis_size("expert")
    groups = lax.axis_size("dp")
    me = lax.axis_index("dp")
    tok_count, model_width = tokens.shape
    pair_count = tok_count * expert_ids.shape[1]
    capacity = 3 * pair_count // (2 * experts)
    half = experts // 2
    capacity = -(-capacity // 16) * 16
    rows = experts * capacity
    width = model_width // CHUNKS
    sel, sel_gate = selection(expert_ids, gate_codes, experts, capacity)
    both = jnp.stack([sel, sel_gate]).reshape(2, 2, half * capacity, tok_count)
    sides = both.transpose(1, 0, 2, 3)
    sides_t = both.transpose(1, 0, 3, 2)
    gate_matrix, up_matrix, down_matrix = w_gate[0], w_up[0], w_down[0]
    hidden_units = gate_matrix.shape[1]
    contract_rows = (((0,), (0,)), ((), ()))
    vmem = pl.BlockSpec(memory_space=pltpu.VMEM)
    anywhere = pl.BlockSpec(memory_space=pl.ANY)
    steps = 2 * CHUNKS
    dma = pltpu.SemaphoreType.DMA
    weights = [
        pltpu.VMEM((model_width, hidden_units), BF16),
        pltpu.VMEM((model_width, hidden_units), BF16),
        pltpu.VMEM((hidden_units, model_width), BF16),
    ]

    def shape(*dims):
        return jax.ShapeDtypeStruct(dims, BF16)

    arrived, incoming, hidden, gate_pre_grad, up_pre_grad, far_sel_t = pl.pallas_call(
        functools.partial(dispatch_kernel, half, capacity),
        out_shape=(
            shape(rows, model_width),
            shape(rows, model_width),
            shape(rows, hidden_units),
            shape(rows, hidden_units),
            shape(rows, hidden_units),
            shape(2, tok_count, half * capacity),
        ),
        in_specs=[vmem] * 4 + [anywhere] * 3,
        out_specs=(vmem,) * 6,
        scratch_shapes=[
            pltpu.VMEM((2, half * capacity, tok_count), BF16),
            pltpu.VMEM((steps, tok_count, width), BF16),
            pltpu.VMEM((steps, 2, half * capacity, width), BF16),
            pltpu.VMEM((rows, hidden_units), F32),
            pltpu.VMEM((rows, hidden_units), F32),
            pltpu.VMEM((rows, hidden_units), F32),
            *weights,
            dma((3,)),
            dma((2,)),
            dma((2,)),
            dma((steps,)),
            dma((steps,)),
            dma((steps, 2, half - 1)),
            dma((steps, 2, half - 1)),
        ],
        compiler_params=pltpu.CompilerParams(
            collective_id=0, has_side_effects=True, vmem_limit_bytes=56 * 2**20
        ),
    )(sides, sides_t, tokens, out_grad, gate_matrix, up_matrix, down_matrix)

    arrived_parts = swap_columns(arrived, groups, me)
    incoming_parts = swap_columns(incoming, groups, me)
    factors = jnp.concatenate([gate_pre_grad, up_pre_grad, hidden], axis=0)
    gathered = lax.all_gather(factors, "dp", axis=0, tiled=False)

    layer_out, tokens_grad = pl.pallas_call(
        functools.partial(return_kernel, half, capacity),
        out_shape=(shape(tok_count, model_width), shape(tok_count, model_width)),
        in_specs=[vmem] * 5 + [anywhere] * 3,
        out_specs=(vmem,) * 2,
        scratch_shapes=[
            pltpu.VMEM((steps, rows, width), BF16),
            pltpu.VMEM((steps, 2, half * capacity, width), BF16),
            pltpu.VMEM((steps, tok_count, width), BF16),
            pltpu.VMEM((steps, tok_count, width), BF16),
            *weights,
            dma((3,)),
            dma((steps,)),
            dma((steps,)),
            dma((steps, 2, half - 1)),
            dma((steps, 2, half - 1)),
        ],
        cost_estimate=pl.CostEstimate(
            flops=8 * rows * model_width * hidden_units, bytes_accessed=300_000_000, transcendentals=0
        ),
        compiler_params=pltpu.CompilerParams(
            collective_id=1, has_side_effects=True, vmem_limit_bytes=56 * 2**20
        ),
    )(sides_t, far_sel_t, hidden, gate_pre_grad, up_pre_grad, gate_matrix, up_matrix, down_matrix)

    gate_sum = up_sum = down_sum = 0.0
    for shift in range(groups):
        source = lax.rem(me - shift + groups, groups)
        factor = factors if shift == 0 else lax.dynamic_index_in_dim(gathered, source, 0, keepdims=False)
        tok, grad = arrived_parts[shift], incoming_parts[shift]
        gate_sum += lax.dot_general(tok, factor[:rows], contract_rows, preferred_element_type=F32)
        up_sum += lax.dot_general(
            tok, factor[rows : 2 * rows], contract_rows, preferred_element_type=F32
        )
        down_sum += lax.dot_general(
            factor[2 * rows :], grad, contract_rows, preferred_element_type=F32
        )
    return (
        layer_out.astype(BF16),
        tokens_grad.astype(BF16),
        gate_sum.astype(BF16)[None],
        up_sum.astype(BF16)[None],
        down_sum.astype(BF16)[None],
    )


def solution(mesh):
    placed = (
        P(("dp", "expert"), None),
        P(("dp", "expert"), None),
        P(("dp", "expert"), None),
        P("expert", None, None),
        P("expert", None, None),
        P("expert", None, None),
        P(("dp", "expert"), None),
    )
    return jax.shard_map(
        per_device,
        mesh=mesh,
        in_specs=placed,
        out_specs=(
            P(("dp", "expert"), None),
            P(("dp", "expert"), None),
            P("expert", "dp", None),
            P("expert", "dp", None),
            P("expert", None, "dp"),
        ),
        check_vma=False,
    )
```

```python
import functools

import jax
import jax.numpy as jnp
from jax import lax
from jax.experimental import pallas as pl
from jax.experimental.pallas import tpu as pltpu
from jax.sharding import PartitionSpec as P

F32 = jnp.float32
BF16 = jnp.bfloat16
CONTRACT = (((1,), (1,)), ((), ()))


def positions(half):
    me = lax.axis_index("expert")
    side = me // half
    local = me - side * half
    base = side * half
    partner = (1 - side) * half + local
    return me, side, local, base, partner


def meet(half, local, base, partner, groups, group):
    barrier = pltpu.get_barrier_semaphore()
    for shift in range(1, groups):
        pl.semaphore_signal(barrier, inc=1, device_id={"dp": lax.rem(group + shift, groups)})
    for j in range(1, half):
        pl.semaphore_signal(barrier, inc=1, device_id={"expert": base + lax.rem(local + j, half)})
    pl.semaphore_signal(barrier, inc=1, device_id={"expert": partner})
    pl.semaphore_wait(barrier, half + groups - 1)


def remote(src, dst, send, recv, peer, axis="expert"):
    return pltpu.make_async_remote_copy(
        src_ref=src, dst_ref=dst, send_sem=send, recv_sem=recv, device_id={axis: peer}
    )


def dispatch_kernel(
    half, cap, groups, chunks,
    sel, sel_t, tokens, out_grad, w_gate, w_up, w_down,
    token_cols, grad_cols, all_hidden, hidden, gate_pre_grad, up_pre_grad, far_sel_t,
    arrived, incoming, far_sel, far_src, stage, pre_gate, pre_up, hidden_grad, vgate, vup, vdown,
    load_sem, sel_send, sel_recv, far_send, far_recv, near_send, near_recv, group_send, group_recv,
):
    me, side, local, base, partner = positions(half)
    group = lax.axis_index("dp")
    width = tokens.shape[1] // chunks
    block = tokens.shape[1] // groups
    per_block = chunks // groups
    steps = 2 * chunks
    loads = [
        pltpu.make_async_copy(a, b, load_sem.at[i])
        for i, (a, b) in enumerate(((w_gate, vgate), (w_up, vup), (w_down, vdown)))
    ]
    meet(half, local, base, partner, groups, group)
    sources = (tokens, out_grad)
    landed = (arrived, incoming)
    sel_copies = [
        remote(sel.at[1 - side], far_sel, sel_send.at[0], sel_recv.at[0], partner),
        remote(sel_t.at[1 - side], far_sel_t, sel_send.at[1], sel_recv.at[1], partner),
    ]
    sel_copies[0].start()

    def block_columns(shift):
        return pl.ds(pl.multiple_of(lax.rem(group + shift, groups) * block, 128), block)

    def columns(q):
        shift, inner = divmod(q % chunks, per_block)
        start = lax.rem(group + shift, groups) * block + inner * width
        return pl.ds(pl.multiple_of(start, 128), width)

    group_copies = []

    def to_group(source, target, shift, kind):
        if shift == 0:
            copy = pltpu.make_async_copy(source, target.at[0], group_send.at[kind, 0])
        else:
            copy = remote(
                source, target.at[shift], group_send.at[kind, shift], group_recv.at[kind, shift],
                lax.rem(group + shift, groups), "dp",
            )
        copy.start()
        group_copies.append((shift, copy))

    far = [
        remote(sources[q // chunks].at[:, columns(q)], far_src.at[q], far_send.at[q], far_recv.at[q], partner)
        for q in range(steps)
    ]
    started = [[] for _ in range(steps)]

    def rows_of(index):
        return pl.ds(pl.multiple_of(index * cap, 16), cap)

    def spread(q, kind, matrix, values, owner):
        part = q // chunks
        slots = jnp.dot(matrix, values, preferred_element_type=F32).astype(BF16)
        stage[q, kind] = slots
        for j in range(1, half):
            peer = lax.rem(local + j, half)
            copy = remote(
                stage.at[q, kind, rows_of(peer)],
                landed[part].at[rows_of(owner), columns(q)],
                near_send.at[q, kind, j - 1],
                near_recv.at[q, kind, j - 1],
                base + peer,
            )
            copy.start()
            started[q].append(copy)
        landed[part][rows_of(owner), columns(q)] = stage[q, kind, rows_of(local)]

    far[0].start()
    for load in loads:
        load.start()
    for s in range(steps + 2):
        if s + 1 < steps:
            far[s + 1].start()
        if s == 0:
            sel_copies[1].start()
        if s < steps:
            part = s // chunks
            spread(s, 0, sel[side, part], sources[part][:, columns(s)], me)
        if 1 <= s <= steps:
            q = s - 1
            if q == 0:
                sel_copies[0].wait_recv()
            far[q].wait_recv()
            spread(q, 1, far_sel[q // chunks], far_src[q], partner)
        if s >= 2:
            q = s - 2
            for copy in started[q]:
                copy.wait_recv()
            part = q // chunks
            rows = landed[part][:, columns(q)]
            if q == 0:
                loads[0].wait()
                loads[1].wait()
            if q == chunks:
                loads[2].wait()
            if (q + 1) % per_block == 0:
                shift = (q % chunks) // per_block
                to_group(landed[part].at[:, block_columns(shift)], (token_cols, grad_cols)[part], shift, part)
            if part == 0:
                for total, matrix in ((pre_gate, vgate), (pre_up, vup)):
                    term = jnp.dot(rows, matrix[columns(q), :], preferred_element_type=F32)
                    total[...] = term if q == 0 else total[...] + term
                if q == chunks - 1:
                    for start in range(0, pre_gate.shape[0], cap):
                        at = pl.ds(start, cap)
                        gate = pre_gate[at, :]
                        hidden[at, :] = (gate * jax.nn.sigmoid(gate) * pre_up[at, :]).astype(BF16)
                    for shift in range(groups):
                        to_group(hidden, all_hidden, shift, 2)
            else:
                term = lax.dot_general(rows, vdown[:, columns(q)], CONTRACT, preferred_element_type=F32)
                hidden_grad[...] = term if q == chunks else hidden_grad[...] + term
    for start in range(0, pre_gate.shape[0], cap):
        at = pl.ds(start, cap)
        gate, up, grad = pre_gate[at, :], pre_up[at, :], hidden_grad[at, :]
        sigmoid = jax.nn.sigmoid(gate)
        silu = gate * sigmoid
        gate_pre_grad[at, :] = (grad * up * sigmoid * (1.0 + gate * (1.0 - sigmoid))).astype(BF16)
        up_pre_grad[at, :] = (grad * silu).astype(BF16)
    for shift, copy in group_copies:
        if shift == 0:
            copy.wait()
        else:
            copy.wait_recv()
            copy.wait_send()
    sel_copies[1].wait_recv()
    for copy in sel_copies + far:
        copy.wait_send()
    for q in range(steps):
        for copy in started[q]:
            copy.wait_send()


def return_kernel(
    half, cap, groups, chunks,
    sel_t, far_sel_t, hidden, gate_pre_grad, up_pre_grad, token_cols, grad_cols, all_hidden,
    w_gate, w_up, w_down,
    layer_out, tokens_grad, gate_sum, up_sum, down_sum, factors,
    stage, back, part_send, part_recv, vgate, vup, vdown, left, right, gate_total, up_total, down_total,
    load_sem, far_send, far_recv, near_send, near_recv, group_send, group_recv, piece_sem,
):
    me, side, local, base, partner = positions(half)
    group = lax.axis_index("dp")
    width = layer_out.shape[1] // chunks
    steps = 2 * chunks
    own = (gate_pre_grad, up_pre_grad)
    rows = half * cap
    loads = [
        pltpu.make_async_copy(a, b, load_sem.at[i])
        for i, (a, b) in enumerate(((w_down, vdown), (w_gate, vgate), (w_up, vup)))
    ]
    for load in loads:
        load.start()
    meet(half, local, base, partner, groups, group)
    group_copies = {}
    for shift in range(1, groups):
        for kind in (0, 1):
            copy = remote(
                own[kind], factors.at[shift, kind], group_send.at[shift, kind], group_recv.at[shift, kind],
                lax.rem(group + shift, groups), "dp",
            )
            copy.start()
            group_copies[shift, kind] = copy

    def piece_loads(i):
        slot, source = i % 2, i % groups
        if i < groups:
            pairs = [(grad_cols.at[source], left.at[slot]), (all_hidden.at[source], right.at[slot, 0])]
        else:
            pairs = [(token_cols.at[source], left.at[slot])]
            for kind in (0, 1):
                held = own[kind] if source == 0 else factors.at[source, kind]
                pairs.append((held, right.at[slot, kind]))
        return [pltpu.make_async_copy(a, b, piece_sem.at[i, n]) for n, (a, b) in enumerate(pairs)]

    def start_piece(i):
        if i > groups:
            for kind in (0, 1):
                group_copies[i % groups, kind].wait_recv()
        copies = piece_loads(i)
        for copy in copies:
            copy.start()
        return copies

    def accumulate(total, result, at, term, i):
        source = i % groups
        if source > 0:
            term = total[at, :] + term
        if source < groups - 1:
            total[at, :] = term
        else:
            result[at, :] = term.astype(BF16)

    def run_piece(i, copies):
        for copy in copies:
            copy.wait()
        slot = i % 2
        rows_first = (((0,), (0,)), ((), ()))
        if i < groups:
            for start in range(0, down_sum.shape[0], 256):
                at = pl.ds(start, 256)
                term = lax.dot_general(right[slot, 0, :, at], left[slot], rows_first, preferred_element_type=F32)
                accumulate(down_total, down_sum, at, term, i)
        else:
            for start in range(0, gate_sum.shape[0], 256):
                at = pl.ds(start, 256)
                for kind, total, result in ((0, gate_total, gate_sum), (1, up_total, up_sum)):
                    term = lax.dot_general(left[slot, :, at], right[slot, kind], rows_first, preferred_element_type=F32)
                    accumulate(total, result, at, term, i)

    when = {1 + g: g for g in range(groups)}
    when.update({chunks + 2 + g: groups + g for g in range(groups)})
    pending = {0: start_piece(0)}
    outs = (layer_out, tokens_grad)

    def columns(q):
        return pl.ds((q % chunks) * width, width)

    def rows_of(index):
        return pl.ds(pl.multiple_of(index * cap, 16), cap)

    far = [
        remote(part_send_ref, part_recv_ref, far_send.at[q], far_recv.at[q], partner)
        for q, (part_send_ref, part_recv_ref) in enumerate(
            (part_send.at[q], part_recv.at[q]) for q in range(steps)
        )
    ]
    started = [([], []) for _ in range(steps)]
    for s in range(steps + 2):
        if s < steps:
            if s == 0:
                loads[0].wait()
            if s == chunks:
                loads[1].wait()
                loads[2].wait()
            if s < chunks:
                made = jnp.dot(hidden[...], vdown[:, columns(s)], preferred_element_type=F32)
            else:
                made = lax.dot_general(gate_pre_grad[...], vgate[columns(s), :], CONTRACT, preferred_element_type=F32)
                made = made + lax.dot_general(
                    up_pre_grad[...], vup[columns(s), :], CONTRACT, preferred_element_type=F32
                )
            slot = s % chunks
            if s >= chunks:
                for copies in started[s - chunks]:
                    for copy in copies:
                        copy.wait_send()
            stage[slot] = made.astype(BF16)
            for kind in (1, 0):
                first = base if kind == 0 else half - base
                for j in range(1, half):
                    peer = lax.rem(local + j, half)
                    copy = remote(
                        stage.at[slot, rows_of(first + peer)],
                        back.at[s, kind, rows_of(local)],
                        near_send.at[s, kind, j - 1],
                        near_recv.at[s, kind, j - 1],
                        base + peer,
                    )
                    copy.start()
                    started[s][kind].append(copy)
                back[s, kind, rows_of(local)] = stage[slot, rows_of(first + local)]
        if 1 <= s <= steps:
            q = s - 1
            for copy in started[q][1]:
                copy.wait_recv()
            part_send[q] = jnp.dot(
                far_sel_t[1 - q // chunks], back[q, 1], preferred_element_type=F32
            ).astype(BF16)
            far[q].start()
        if s in when:
            i = when[s]
            if i + 1 < 2 * groups and i + 1 != groups + 1:
                pending[i + 1] = start_piece(i + 1)
            if i not in pending:
                pending[i] = start_piece(i)
            run_piece(i, pending[i])
        if s >= 2:
            q = s - 2
            for copy in started[q][0]:
                copy.wait_recv()
            near = jnp.dot(sel_t[side, 1 - q // chunks], back[q, 0], preferred_element_type=F32)
            far[q].wait_recv()
            outs[q // chunks][:, columns(q)] = (near + part_recv[q].astype(F32)).astype(BF16)
    for copy in far:
        copy.wait_send()
    for q in range(chunks, steps):
        for copies in started[q]:
            for copy in copies:
                copy.wait_send()
    for copy in group_copies.values():
        copy.wait_send()


def selection(expert_ids, gate_codes, experts, capacity):
    tok_count = expert_ids.shape[0]
    expert_range = jnp.arange(experts, dtype=jnp.int32)
    named = expert_ids[:, :, None] == expert_range[None, None, :]
    chosen = jnp.any(named, axis=1).T
    gates = jnp.sum(jnp.where(named, gate_codes[:, :, None], 0), axis=1).T
    gates = gates.astype(jnp.float32) * (1.0 / 64.0)
    earlier = (
        jnp.arange(tok_count, dtype=jnp.int32)[:, None] < jnp.arange(tok_count, dtype=jnp.int32)[None, :]
    )
    ranks = jnp.dot(
        chosen.astype(jnp.bfloat16), earlier.astype(jnp.bfloat16), preferred_element_type=jnp.float32
    ).astype(jnp.int32)
    slots = jnp.where(chosen, ranks, -1)
    hit = slots[:, None, :] == jnp.arange(capacity, dtype=jnp.int32)[None, :, None]
    sel = hit.astype(jnp.bfloat16).reshape(experts * capacity, tok_count)
    sel_gate = jnp.where(hit, gates[:, None, :], 0.0).astype(jnp.bfloat16)
    return sel, sel_gate.reshape(experts * capacity, tok_count)


def per_device(tokens, expert_ids, gate_codes, w_gate, w_up, w_down, out_grad):
    experts = lax.axis_size("expert")
    groups = lax.axis_size("dp")
    tok_count, model_width = tokens.shape
    pair_count = tok_count * expert_ids.shape[1]
    capacity = 3 * pair_count // (2 * experts)
    half = experts // 2
    capacity = -(-capacity // 16) * 16
    rows = experts * capacity
    chunks = groups * max(1, 8 // groups)
    width = model_width // chunks
    block = model_width // groups
    sel, sel_gate = selection(expert_ids, gate_codes, experts, capacity)
    both = jnp.stack([sel, sel_gate]).reshape(2, 2, half * capacity, tok_count)
    sides = both.transpose(1, 0, 2, 3)
    sides_t = both.transpose(1, 0, 3, 2)
    gate_matrix, up_matrix, down_matrix = w_gate[0], w_up[0], w_down[0]
    hidden_units = gate_matrix.shape[1]
    vmem = pl.BlockSpec(memory_space=pltpu.VMEM)
    anywhere = pl.BlockSpec(memory_space=pl.ANY)
    steps = 2 * chunks
    dma = pltpu.SemaphoreType.DMA
    weights = [
        pltpu.VMEM((model_width, hidden_units), BF16),
        pltpu.VMEM((model_width, hidden_units), BF16),
        pltpu.VMEM((hidden_units, model_width), BF16),
    ]

    def shape(*dims):
        return jax.ShapeDtypeStruct(dims, BF16)

    token_cols, grad_cols, all_hidden, hidden, gate_pre_grad, up_pre_grad, far_sel_t = pl.pallas_call(
        functools.partial(dispatch_kernel, half, capacity, groups, chunks),
        out_shape=(
            shape(groups, rows, block),
            shape(groups, rows, block),
            shape(groups, rows, hidden_units),
            shape(rows, hidden_units),
            shape(rows, hidden_units),
            shape(rows, hidden_units),
            shape(2, tok_count, half * capacity),
        ),
        in_specs=[vmem] * 4 + [anywhere] * 3,
        out_specs=(anywhere,) * 3 + (vmem,) * 4,
        scratch_shapes=[
            pltpu.VMEM((rows, model_width), BF16),
            pltpu.VMEM((rows, model_width), BF16),
            pltpu.VMEM((2, half * capacity, tok_count), BF16),
            pltpu.VMEM((steps, tok_count, width), BF16),
            pltpu.VMEM((steps, 2, half * capacity, width), BF16),
            pltpu.VMEM((rows, hidden_units), F32),
            pltpu.VMEM((rows, hidden_units), F32),
            pltpu.VMEM((rows, hidden_units), F32),
            *weights,
            dma((3,)),
            dma((2,)),
            dma((2,)),
            dma((steps,)),
            dma((steps,)),
            dma((steps, 2, half - 1)),
            dma((steps, 2, half - 1)),
            dma((3, groups)),
            dma((3, groups)),
        ],
        compiler_params=pltpu.CompilerParams(
            collective_id=0, has_side_effects=True, vmem_limit_bytes=56 * 2**20
        ),
    )(sides, sides_t, tokens, out_grad, gate_matrix, up_matrix, down_matrix)

    layer_out, tokens_grad, gate_sum, up_sum, down_sum, _ = pl.pallas_call(
        functools.partial(return_kernel, half, capacity, groups, chunks),
        out_shape=(
            shape(tok_count, model_width),
            shape(tok_count, model_width),
            shape(block, hidden_units),
            shape(block, hidden_units),
            shape(hidden_units, block),
            shape(groups, 2, rows, hidden_units),
        ),
        in_specs=[vmem] * 5 + [anywhere] * 6,
        out_specs=(vmem,) * 5 + (anywhere,),
        scratch_shapes=[
            pltpu.VMEM((chunks, rows, width), BF16),
            pltpu.VMEM((steps, 2, half * capacity, width), BF16),
            pltpu.VMEM((steps, tok_count, width), BF16),
            pltpu.VMEM((steps, tok_count, width), BF16),
            *weights,
            pltpu.VMEM((2, rows, block), BF16),
            pltpu.VMEM((2, 2, rows, hidden_units), BF16),
            pltpu.VMEM((block, hidden_units), F32),
            pltpu.VMEM((block, hidden_units), F32),
            pltpu.VMEM((hidden_units, block), F32),
            dma((3,)),
            dma((steps,)),
            dma((steps,)),
            dma((steps, 2, half - 1)),
            dma((steps, 2, half - 1)),
            dma((groups, 2)),
            dma((groups, 2)),
            dma((2 * groups, 3)),
        ],
        compiler_params=pltpu.CompilerParams(
            collective_id=1, has_side_effects=True, vmem_limit_bytes=63 * 2**20
        ),
    )(
        sides_t, far_sel_t, hidden, gate_pre_grad, up_pre_grad, token_cols, grad_cols, all_hidden,
        gate_matrix, up_matrix, down_matrix,
    )
    return layer_out, tokens_grad, gate_sum[None], up_sum[None], down_sum[None]


def solution(mesh):
    placed = (
        P(("dp", "expert"), None),
        P(("dp", "expert"), None),
        P(("dp", "expert"), None),
        P("expert", None, None),
        P("expert", None, None),
        P("expert", None, None),
        P(("dp", "expert"), None),
    )
    return jax.shard_map(
        per_device,
        mesh=mesh,
        in_specs=placed,
        out_specs=(
            P(("dp", "expert"), None),
            P(("dp", "expert"), None),
            P("expert", "dp", None),
            P("expert", "dp", None),
            P("expert", None, "dp"),
        ),
        check_vma=False,
    )
```
